32 devices in a mesh: member: 4 (over y, x), slab: 2 (over core), tile: 4 (over z).
Axes of the slice: x: 2, y: 2, z: 4, core: 2. Of those that a mesh axis runs over, the one named last changes fastest.
Arguments:
- prior: float32 [128, 32768], P('member', ('slab', 'tile')), may hold values from -6 to 6
- sensitivity: bfloat16 [64, 16, 64, 512], P(('slab', 'tile')), may hold values from -0.0625 to 0.0625
- pattern: int32 [64, 16], P(('slab', 'tile')), may hold values from -1 to 63, as said below
- ownership: int32 [64], replicated, may hold values from 0 to 63, each once
- observed: float32 [4096], P(('slab', 'tile')), may hold values from -8 to 8
- obs_noise: float32 [4096], P(('slab', 'tile')), may hold values from 0.3 to 3
- perturbation: float32 [128, 4096], P('member', ('slab', 'tile')), may hold values from -5 to 5
Outputs:
- increment: float32 [128, 32768], P('member', ('slab', 'tile'))
- weights: float32 [128, 128], replicated
The draws below stay inside these ranges and needn't reach their ends.
Inputs may be any that keep to these rules, and one draw needn't show every extreme that they name: In each row of pattern the first c entries are distinct observation block numbers and the remaining 16 - c entries are -1, with 4 <= c <= 16; some row is full and some row has exactly 4 live entries.
All inputs are finite; a program needn't handle non-finite values.
Results may differ from the reference program's by a relative error of at most 0.0042.
Values may be sent and summed in bfloat16 or wider, within the bound.
No kernel may reach another device: no remote copies, remote signals or barrier semaphores. Data moves between devices by JAX's collectives and lax.ppermute only.
A program may use at most 64 MiB of HBM per device.

```python
import math
import jax
import jax.numpy as jnp
from jax import lax

NE = 128
OBS_BLOCK = 64
PB = 512
KB = 16
NPB = 8
OBLK_DEV = 8
NPBT = 64
P_SIZE = 32768
NBLK = 64
M = 4096
N_SLAB = 2
N_TILE = 4


def draw_pattern(key, part):
    row_total = NPB * N_SLAB * N_TILE
    block_total = OBLK_DEV * N_SLAB * N_TILE
    order_key = jax.random.fold_in(key, 11)
    count_key = jax.random.fold_in(key, 12)
    head_key = jax.random.fold_in(key, 13)
    row_keys = jax.random.split(order_key, row_total)
    chosen = jax.vmap(lambda row_key: jax.random.permutation(row_key, block_total)[:KB])(row_keys)
    chosen = chosen.astype(jnp.int32)
    head_row = jnp.concatenate([jnp.full((1,), block_total - 1, jnp.int32), jax.random.permutation(head_key, block_total - 1)[:KB - 1].astype(jnp.int32)])
    chosen = chosen.at[0].set(head_row)
    counts = jax.random.randint(count_key, (row_total,), KB // 4, KB + 1)
    counts = counts.at[0].set(KB).at[row_total - 1].set(KB // 4)
    position = jnp.arange(KB)[None, :]
    return jnp.where(position < counts[:, None], chosen, -1).astype(jnp.int32)


def draw_observed(key, part):
    obs_total = OBLK_DEV * N_SLAB * N_TILE * OBS_BLOCK
    ramp = 0.6 + 1.2 * jnp.arange(obs_total, dtype=jnp.float32) / obs_total
    values = jnp.clip(jax.random.normal(key, (obs_total,), jnp.float32), -4.0, 4.0)
    return (ramp * values).astype(jnp.float32)


def shard_levels(rng, extent, pieces, smallest, largest):
    loudness, own = 1.0, jax.random.fold_in(rng, 6)
    for axis_at, blocks in pieces:
        heights = jnp.exp(jax.random.uniform(jax.random.fold_in(own, axis_at), (blocks,), jnp.float32, smallest / len(pieces), largest / len(pieces)))
        loudness = loudness * jnp.repeat(heights, extent[axis_at] // blocks).reshape([-1 if axis == axis_at else 1 for axis in range(len(extent))])
    return loudness


def scatter_about(stream_key, dims, scale, most, cuts=(), kind=jnp.bfloat16):
    drawn = scale * jax.random.normal(stream_key, dims, jnp.float32)
    if cuts:
        drawn = drawn * shard_levels(stream_key, dims, cuts, -0.22, 0.18)
    return jnp.clip(drawn, -most, most).astype(kind)


def setup_inputs(seed: int = 0) -> dict:
    key_of = jax.random.split(jax.random.key(seed), 8)
    prior = scatter_about(key_of[0], (NE, P_SIZE), 1.0, 6.0, ((0, 4), (1, 8)), jnp.float32)
    sensitivity = scatter_about(key_of[1], (NPBT, KB, OBS_BLOCK, PB), (PB * NPB * KB // OBLK_DEV) ** -0.5, 0.0625, ((0, 8),))
    pattern = draw_pattern(jax.random.fold_in(key_of[7], 71), 0)
    ownership = jax.random.permutation(key_of[3], NBLK).astype(jnp.int32)
    observed = draw_observed(jax.random.fold_in(key_of[7], 71), 0)
    obs_noise = jnp.clip(jnp.exp(math.log(3.0) - 2.3025851 * jax.random.uniform(key_of[5], (M,), jnp.float32) ** shard_levels(key_of[5], (M,), ((0, 8),), -0.2, 0.2)), 0.3, 3.0)
    perturbation = scatter_about(key_of[6], (NE, M), 1.0, 5.0, ((0, 4), (1, 8)), jnp.float32)
    return dict(prior=prior, sensitivity=sensitivity, pattern=pattern, ownership=ownership, observed=observed, obs_noise=obs_noise, perturbation=perturbation)


def reference(prior, sensitivity, pattern, ownership, observed, obs_noise, perturbation):
    group_count = N_SLAB * N_TILE
    prior_bf = prior.astype(jnp.bfloat16)
    shaped = prior_bf.reshape(NE, group_count, NPB, PB).transpose(1, 0, 2, 3)
    sens_groups = sensitivity.reshape(group_count, NPB, KB, OBS_BLOCK, PB)
    pattern_groups = pattern.reshape(group_count, NPB * KB)

    def accumulate_group(carry, item):
        prior_group, sens_group, pattern_group = item
        contrib = jnp.einsum('bkop,mbp->mbko', sens_group.astype(jnp.float32), prior_group.astype(jnp.float32), precision=lax.Precision.HIGHEST)
        contrib = contrib.reshape(NE, NPB * KB, OBS_BLOCK)
        onehot = (pattern_group[:, None] == ownership[None, :]).astype(jnp.float32)
        placed = jnp.einsum('mjo,js->mso', contrib, onehot, precision=lax.Precision.HIGHEST)
        return (carry + placed, None)
    start_value = jnp.zeros((NE, NBLK, OBS_BLOCK), jnp.float32)
    predicted, _ = lax.scan(accumulate_group, start_value, (shaped, sens_groups, pattern_groups))
    predicted = predicted.reshape(NE, M)
    norm_scale = 1.0 / math.sqrt(NE - 1)
    mean_pred = lax.optimization_barrier(jnp.mean(predicted, axis=0))
    spread = (predicted - mean_pred) * norm_scale / obs_noise
    innovation = (observed - predicted) / obs_noise + perturbation
    gram_matrix = jnp.einsum('mo,ko->mk', spread, spread, precision=lax.Precision.HIGHEST)
    cross_term = jnp.einsum('mo,ko->mk', spread, innovation, precision=lax.Precision.HIGHEST)
    misfit = jnp.sum(innovation * innovation)
    damping = misfit / (4.0 * NE * NE)
    system = gram_matrix + damping * jnp.eye(NE, dtype=jnp.float32)
    factor = jnp.linalg.cholesky(system)
    weights = jax.scipy.linalg.cho_solve((factor, True), cross_term)
    centred = ((weights - lax.optimization_barrier(jnp.mean(weights, axis=0, keepdims=True))) * norm_scale).astype(jnp.bfloat16)
    increment = lax.dot_general(centred.astype(jnp.float32), prior_bf.astype(jnp.float32), (((0,), (0,)), ((), ())), preferred_element_type=jnp.float32)
    return (increment, weights)
```

```python
import math

import jax
import jax.numpy as jnp
from jax import lax
from jax.sharding import PartitionSpec as P


def swap(x, axis, distance):
    size = lax.axis_size(axis)
    return lax.ppermute(x, axis, [(i, i ^ distance) for i in range(size)])


def digits(size):
    out, shift = [], 0
    while size > 1:
        radix = 4 if size % 4 == 0 else 2
        out.append((shift, radix))
        shift += radix.bit_length() - 1
        size //= radix
    return out[::-1]


def scatter_sum(chunks, axis):
    for shift, radix in digits(lax.axis_size(axis)):
        low = 1 << shift
        got = [
            [swap(chunks[d * low + r], axis, d << shift) for r in range(low)]
            for d in range(1, radix)
        ]
        chunks = [sum((g[r] for g in got), chunks[r]) for r in range(low)]
    return chunks[0]


def all_sum(x, axis):
    for shift, radix in digits(lax.axis_size(axis))[::-1]:
        x = sum((swap(x, axis, d << shift) for d in range(1, radix)), x)
    return x


def gather_xor(x, axis):
    return [x] + [swap(x, axis, r) for r in range(1, lax.axis_size(axis))]


def ordered(parts, index):
    stacked = jnp.stack(parts)
    return jnp.take(stacked, jnp.arange(len(parts)) ^ index, axis=0).reshape(
        len(parts) * parts[0].shape[0], *parts[0].shape[1:]
    )


def local(prior, sensitivity, pattern, ownership, observed, obs_noise, perturbation):
    members_dev = prior.shape[0]
    members = members_dev * lax.axis_size("member")
    blocks_dev, slot_count, obs_block, block_params = sensitivity.shape
    block_total = ownership.shape[0]
    obs_dev = observed.shape[0]
    owned_blocks = obs_dev // obs_block
    tiles = lax.axis_size("tile")
    norm_scale = 1.0 / math.sqrt(members - 1)
    member_at = lax.axis_index("member")
    slab_at = lax.axis_index("slab")
    tile_at = lax.axis_index("tile")
    prior_bf = prior.astype(jnp.bfloat16)

    shaped = prior_bf.reshape(members_dev, blocks_dev, block_params)
    contrib = jnp.einsum("bkop,mbp->bkmo", sensitivity, shaped, preferred_element_type=jnp.float32)
    contrib_rows = contrib.reshape(blocks_dev * slot_count, members_dev * obs_block)
    flat_pattern = pattern.reshape(blocks_dev * slot_count)
    storage_of = (
        jnp.zeros((block_total,), jnp.int32)
        .at[ownership]
        .set(jnp.arange(block_total, dtype=jnp.int32))
    )
    row = storage_of[jnp.maximum(flat_pattern, 0)]
    row = row ^ ((slab_at * tiles + tile_at) * owned_blocks)
    target = jnp.where(flat_pattern >= 0, row, block_total)
    placed = (
        jnp.zeros((block_total + 1, members_dev * obs_block), jnp.float32)
        .at[target]
        .add(contrib_rows)
    )
    half = tiles * owned_blocks
    chip = placed[:half] + swap(placed[half : 2 * half], "slab", 1)
    own = scatter_sum(
        [chip[r * owned_blocks : (r + 1) * owned_blocks] for r in range(tiles)], "tile"
    )
    predicted = (
        own.reshape(owned_blocks, members_dev, obs_block)
        .transpose(1, 0, 2)
        .reshape(members_dev, obs_dev)
    )
    noise_all = ordered(gather_xor(perturbation, "member"), member_at)
    predicted = ordered(gather_xor(predicted, "member"), member_at)
    mean_pred = jnp.mean(predicted, axis=0)
    spread = (predicted - mean_pred) * norm_scale / obs_noise
    innovation = (observed - predicted) / obs_noise + noise_all
    gram = jnp.einsum("mo,ko->mk", spread, spread, precision=lax.Precision.HIGHEST)
    cross = jnp.einsum("mo,ko->mk", spread, innovation, precision=lax.Precision.HIGHEST)
    misfit = jnp.sum(innovation * innovation)
    gram = gram + misfit / (4.0 * members * members) * jnp.eye(members, dtype=jnp.float32)
    both = jnp.concatenate([gram, cross], axis=1)
    rows = members // 2
    mine = lax.dynamic_slice_in_dim(both, slab_at * rows, rows, 0)
    other = lax.dynamic_slice_in_dim(both, (1 - slab_at) * rows, rows, 0)
    mine = all_sum(mine + swap(other, "slab", 1), "tile")
    both = ordered([mine, swap(mine, "slab", 1)], slab_at)
    system, cross = both[:, :members], both[:, members:]
    factor = jnp.linalg.cholesky(system)
    weights = jax.scipy.linalg.cho_solve((factor, True), cross)
    centred = ((weights - jnp.mean(weights, axis=0, keepdims=True)) * norm_scale).astype(
        jnp.bfloat16
    )
    own_cols = lax.dynamic_slice_in_dim(centred, member_at * members_dev, members_dev, 1)
    increment = lax.dot_general(
        own_cols,
        ordered(gather_xor(prior_bf, "member"), member_at),
        (((0,), (0,)), ((), ())),
        preferred_element_type=jnp.float32,
    )
    return (increment, weights)


def solution(mesh):
    return jax.shard_map(
        local,
        mesh=mesh,
        in_specs=(
            P("member", ("slab", "tile")),
            P(("slab", "tile"), None, None, None),
            P(("slab", "tile"), None),
            P(),
            P(("slab", "tile")),
            P(("slab", "tile")),
            P("member", ("slab", "tile")),
        ),
        out_specs=(P("member", ("slab", "tile")), P()),
        check_vma=False,
    )
```

```python
import functools
import math

import jax
import jax.numpy as jnp
from jax import lax
from jax.experimental import pallas as pl
from jax.experimental.pallas import tpu as pltpu
from jax.sharding import PartitionSpec as P

EXACT = lax.Precision.HIGHEST
VMEM = pl.BlockSpec(memory_space=pltpu.VMEM)
SMEM = pl.BlockSpec(memory_space=pltpu.SMEM)
NT = (((1,), (1,)), ((), ()))


def swap(x, axis, distance):
    size = lax.axis_size(axis)
    return lax.ppermute(x, axis, [(i, i ^ distance) for i in range(size)])


def digits(size):
    out, shift = [], 0
    while size > 1:
        radix = 4 if size % 4 == 0 else 2
        out.append((shift, radix))
        shift += radix.bit_length() - 1
        size //= radix
    return out[::-1]


def gather_xor(x, axis):
    return [x] + [swap(x, axis, r) for r in range(1, lax.axis_size(axis))]


def contribute_kernel(
    owned, pattern_ref, ownership_ref, prior_ref, sens_ref, keep_ref, send_ref, bf_ref, acc, storage
):
    step = pl.program_id(0)
    tiles, members_dev, obs_dev = keep_ref.shape
    _, slots, obs_block, params = sens_ref.shape
    total = ownership_ref.shape[0]
    me = lax.axis_index("slab") * tiles + lax.axis_index("tile")

    @pl.when(step == 0)
    def _():
        def place(s, carry):
            storage[ownership_ref[s]] = s ^ (me * owned)
            return carry

        lax.fori_loop(0, total, place, 0, unroll=8)
        acc[...] = jnp.zeros_like(acc)

    rows = prior_ref[...].astype(jnp.bfloat16)
    bf_ref[...] = rows
    terms = lax.dot_general(
        rows, sens_ref[0].reshape(slots * obs_block, params), NT, preferred_element_type=jnp.float32
    )
    for k in range(slots):
        block = pattern_ref[step, k]
        at = jnp.where(block >= 0, storage[jnp.maximum(block, 0)], total)
        acc[at] += terms[:, k * obs_block : (k + 1) * obs_block]

    @pl.when(step == pl.num_programs(0) - 1)
    def _():
        group = max(1, 128 // obs_block)

        def flush(r, carry):
            for out, base in ((keep_ref, 0), (send_ref, tiles * owned)):
                for q in range(owned // group):
                    first = base + r * owned + q * group
                    out[r, :, q * group * obs_block : (q + 1) * group * obs_block] = (
                        jnp.concatenate([acc[first + g] for g in range(group)], axis=1)
                    )
            return carry

        lax.fori_loop(0, tiles, flush, 0)


def contribute(prior, sensitivity, pattern, ownership, obs_dev):
    members_dev = prior.shape[0]
    blocks, slots, obs_block, params = sensitivity.shape
    total = ownership.shape[0]
    tiles = lax.axis_size("tile")
    owned = obs_dev // obs_block
    half = jax.ShapeDtypeStruct((tiles, members_dev, obs_dev), jnp.float32)
    return pl.pallas_call(
        functools.partial(contribute_kernel, owned),
        grid_spec=pltpu.PrefetchScalarGridSpec(
            num_scalar_prefetch=2,
            grid=(blocks,),
            in_specs=[
                pl.BlockSpec((members_dev, params), lambda b, *_: (0, b)),
                pl.BlockSpec((1, slots, obs_block, params), lambda b, *_: (b, 0, 0, 0)),
            ],
            out_specs=[
                pl.BlockSpec(half.shape, lambda b, *_: (0, 0, 0)),
                pl.BlockSpec(half.shape, lambda b, *_: (0, 0, 0)),
                pl.BlockSpec((members_dev, params), lambda b, *_: (0, b)),
            ],
            scratch_shapes=[
                pltpu.VMEM((total + 1, members_dev, obs_block), jnp.float32),
                pltpu.SMEM((total,), jnp.int32),
            ],
        ),
        out_shape=[half, half, jax.ShapeDtypeStruct(prior.shape, jnp.bfloat16)],
        name="contribute",
    )(pattern, ownership, prior, sensitivity)


def gram_kernel(count, *refs):
    predicted, noise = refs[:count], refs[count : 2 * count]
    observed, sigma, keep, send, stack, whole = refs[2 * count :]
    members_dev = predicted[0].shape[0]
    members = members_dev * count
    at = lax.axis_index("member")
    for r in range(count):
        rows = pl.ds(pl.multiple_of((at ^ r) * members_dev, members_dev), members_dev)
        stack[rows, :] = predicted[r][...]
        whole_rows = pl.ds(pl.multiple_of(members + (at ^ r) * members_dev, members_dev), members_dev)
        stack[whole_rows, :] = noise[r][...]
    values = stack[:members, :]
    inverse = 1.0 / sigma[...]
    spread = (values - jnp.mean(values, axis=0, keepdims=True)) * (
        inverse * (1.0 / math.sqrt(members - 1))
    )
    innovation = (observed[...] - values) * inverse + stack[members:, :]
    stack[:members, :] = spread
    stack[members:, :] = innovation
    misfit = jnp.sum(jnp.sum(innovation * innovation, axis=0, keepdims=True), axis=1, keepdims=True)
    both = lax.dot_general(
        spread, stack[...], NT, precision=EXACT, preferred_element_type=jnp.float32
    )
    row = lax.broadcasted_iota(jnp.int32, both.shape, 0)
    col = lax.broadcasted_iota(jnp.int32, both.shape, 1)
    whole[...] = both + jnp.where(row == col, misfit * (1.0 / (4.0 * members * members)), 0.0)
    rows = members // 2
    side = lax.axis_index("slab")
    keep[...] = whole[pl.ds(pl.multiple_of(side * rows, rows), rows), :]
    send[...] = whole[pl.ds(pl.multiple_of((1 - side) * rows, rows), rows), :]


def gram(predicted, noise, observed, sigma):
    count = len(predicted)
    members_dev, obs_dev = predicted[0].shape
    members = members_dev * count
    half = jax.ShapeDtypeStruct((members // 2, 2 * members), jnp.float32)
    return pl.pallas_call(
        functools.partial(gram_kernel, count),
        in_specs=[VMEM] * (2 * count + 2),
        out_specs=[VMEM, VMEM],
        out_shape=[half, half],
        scratch_shapes=[
            pltpu.VMEM((2 * members, obs_dev), jnp.float32),
            pltpu.VMEM((members, 2 * members), jnp.float32),
        ],
        name="gram",
    )(*predicted, *noise, observed.reshape(1, obs_dev), sigma.reshape(1, obs_dev))


def update_kernel(count, *refs):
    mine, other = refs[:2]
    prior = refs[2 : 2 + count]
    increment, weights, both, cols, ensemble, sems = refs[2 + count :]
    members = weights.shape[0]
    members_dev = members // count
    at = lax.axis_index("member")
    side = lax.axis_index("slab")
    copies = []
    for r in range(count):
        rows = pl.ds(pl.multiple_of((at ^ r) * members_dev, members_dev), members_dev)
        copies.append(pltpu.make_async_copy(prior[r], ensemble.at[rows, :], sems.at[r]))
        copies[-1].start()
    half = members // 2
    both[pl.ds(pl.multiple_of(side * half, half), half), :] = mine[...]
    both[pl.ds(pl.multiple_of((1 - side) * half, half), half), :] = other[...]
    row = lax.broadcasted_iota(jnp.int32, (members, members), 0)
    col = lax.broadcasted_iota(jnp.int32, (members, members), 1)
    eye = jnp.where(row == col, 1.0, 0.0)
    system = both[:, :members]

    def total(x):
        return jnp.sum(jnp.sum(x, axis=0, keepdims=True), axis=1, keepdims=True)

    trace = total(system * eye)
    system = system + trace * (1.0 / (members * members))
    bound = jnp.max(jnp.sum(jnp.abs(system), axis=0, keepdims=True), axis=1, keepdims=True)
    scale = jnp.minimum(trace * (1.0 + 1.0 / members) / total(system * system), 1.9 / bound)
    power = eye - scale * system
    terms = both[:, members:] * scale

    def step(power, terms):
        pair = lax.dot_general(
            power,
            jnp.concatenate([power, terms], axis=1),
            (((1,), (0,)), ((), ())),
            precision=EXACT,
            preferred_element_type=jnp.float32,
        )
        return pair[:, :members], terms + pair[:, members:]

    for _ in range(5):
        power, terms = step(power, terms)

    def unfinished(carry):
        power, _, count = carry
        return (jnp.sum(power * power) > 1e-12) & (count < 40)

    def further(carry):
        power, terms, count = carry
        power, terms = step(power, terms)
        return power, terms, count + 1

    _, terms, _ = lax.while_loop(unfinished, further, (power, terms, 0))
    weights[...] = terms
    centred = (terms - jnp.mean(terms, axis=0, keepdims=True)) * (1.0 / math.sqrt(members - 1))
    cols[...] = centred.T
    own = cols[pl.ds(pl.multiple_of(at * members_dev, members_dev), members_dev), :].astype(
        jnp.bfloat16
    )
    for copy in copies:
        copy.wait()
    width = 512

    def multiply(n, carry):
        lanes = pl.ds(pl.multiple_of(n * width, width), width)
        increment[:, lanes] = jnp.dot(own, ensemble[:, lanes], preferred_element_type=jnp.float32)
        return carry

    lax.fori_loop(0, increment.shape[1] // width, multiply, 0, unroll=True)


def update(mine, other, prior):
    count = len(prior)
    members_dev, params = prior[0].shape
    members = members_dev * count
    return pl.pallas_call(
        functools.partial(update_kernel, count),
        in_specs=[VMEM, VMEM] + [pl.BlockSpec(memory_space=pl.ANY)] * count,
        out_specs=[VMEM, VMEM],
        out_shape=[
            jax.ShapeDtypeStruct((members_dev, params), jnp.float32),
            jax.ShapeDtypeStruct((members, members), jnp.float32),
        ],
        scratch_shapes=[
            pltpu.VMEM((members, 2 * members), jnp.float32),
            pltpu.VMEM((members, members), jnp.float32),
            pltpu.VMEM((members, params), jnp.bfloat16),
            pltpu.SemaphoreType.DMA((count,)),
        ],
        name="update",
    )(mine, other, *prior)


def local(prior, sensitivity, pattern, ownership, observed, obs_noise, perturbation):
    obs_dev = observed.shape[0]
    tiles = lax.axis_size("tile")
    keep, send, prior_bf = contribute(prior, sensitivity, pattern, ownership, obs_dev)
    got = swap(send, "slab", 1)
    chunks = [keep[r] + got[r] for r in range(tiles)]
    chunks, perturbation = lax.optimization_barrier((chunks, perturbation))
    noise = gather_xor(perturbation, "member")
    for shift, radix in digits(tiles):
        low = 1 << shift
        arrived = [
            [swap(chunks[d * low + r], "tile", d << shift) for r in range(low)]
            for d in range(1, radix)
        ]
        chunks = [sum((g[r] for g in arrived), chunks[r]) for r in range(low)]
    predicted = gather_xor(chunks[0], "member")
    keep, send = gram(predicted, noise, observed, obs_noise)
    keep, send, prior_bf = lax.optimization_barrier((keep, send, prior_bf))
    mine = keep + swap(send, "slab", 1)
    mine, prior_bf = lax.optimization_barrier((mine, prior_bf))
    ensemble = gather_xor(prior_bf, "member")
    for shift, radix in digits(tiles)[::-1]:
        mine = sum((swap(mine, "tile", d << shift) for d in range(1, radix)), mine)
    return tuple(update(mine, swap(mine, "slab", 1), ensemble))


def solution(mesh):
    return jax.shard_map(
        local,
        mesh=mesh,
        in_specs=(
            P("member", ("slab", "tile")),
            P(("slab", "tile"), None, None, None),
            P(("slab", "tile"), None),
            P(),
            P(("slab", "tile")),
            P(("slab", "tile")),
            P("member", ("slab", "tile")),
        ),
        out_specs=(P("member", ("slab", "tile")), P()),
        check_vma=False,
    )
```

```python
import functools
import math

import jax
import jax.numpy as jnp
from jax import lax
from jax.experimental import pallas as pl
from jax.experimental.pallas import tpu as pltpu
from jax.sharding import PartitionSpec as P


EXACT = lax.Precision.HIGHEST
VMEM = pl.BlockSpec(memory_space=pltpu.VMEM)
SMEM = pl.BlockSpec(memory_space=pltpu.SMEM)
NT = (((1,), (1,)), ((), ()))


def swap(x, axis, distance):
    size = lax.axis_size(axis)
    return lax.ppermute(x, axis, [(i, i ^ distance) for i in range(size)])


def digits(size):
    out, shift = [], 0
    while size > 1:
        radix = 4 if size % 4 == 0 else 2
        out.append((shift, radix))
        shift += radix.bit_length() - 1
        size //= radix
    return out[::-1]


def gather_xor(x, axis):
    return [x] + [swap(x, axis, r) for r in range(1, lax.axis_size(axis))]


def contribute_kernel(
    owned,
    depth,
    pattern_ref,
    ownership_ref,
    prior_hbm,
    sens_hbm,
    keep_ref,
    send_ref,
    bf_ref,
    sens,
    prior,
    acc,
    storage,
    sens_sems,
    prior_sems,
):
    blocks, slots = pattern_ref.shape
    tiles, _, lanes = keep_ref.shape
    members_dev = prior.shape[0]
    _, rows_block, params = sens.shape
    obs_block = rows_block // slots
    copies = lanes // members_dev
    groups = owned // copies
    me = lax.axis_index("slab") * tiles + lax.axis_index("tile")

    def cols(b):
        return pl.ds(pl.multiple_of(b * params, params), params)

    def fetch(b):
        return (
            pltpu.make_async_copy(prior_hbm.at[:, cols(b)], prior.at[:, cols(b)], prior_sems.at[b]),
            pltpu.make_async_copy(sens_hbm.at[b], sens.at[b], sens_sems.at[b]),
        )

    for b in range(depth):
        for copy in fetch(b):
            copy.start()

    def place(s, carry):
        storage[ownership_ref[s]] = s ^ (me * owned)
        return carry

    lax.fori_loop(0, ownership_ref.shape[0], place, 0, unroll=8)
    acc[...] = jnp.zeros_like(acc)
    lane_group = lax.broadcasted_iota(jnp.int32, (obs_block, lanes), 1) // members_dev

    def work(b, carry):
        @pl.when(b + depth < blocks)
        def _():
            for copy in fetch(b + depth):
                copy.start()

        for copy in fetch(b):
            copy.wait()
        rows = prior[:, cols(b)].astype(jnp.bfloat16)
        bf_ref[:, cols(b)] = rows
        terms = lax.dot_general(
            sens[b],
            jnp.concatenate([rows] * copies, axis=0),
            NT,
            preferred_element_type=jnp.float32,
        )
        for k in range(slots):
            block = pattern_ref[b, k]
            at = storage[jnp.maximum(block, 0)]
            group = jnp.where(block >= 0, (at % owned) // groups, -1)
            acc[(at // owned) * groups + at % groups] += jnp.where(
                lane_group == group, terms[k * obs_block : (k + 1) * obs_block], 0.0
            )
        return carry

    lax.fori_loop(0, blocks, work, 0)

    def flush(r, carry):
        for g in range(groups):
            rows = slice(g * obs_block, (g + 1) * obs_block)
            keep_ref[r, rows, :] = acc[r * groups + g]
            send_ref[r, rows, :] = acc[(tiles + r) * groups + g]
        return carry

    lax.fori_loop(0, tiles, flush, 0, unroll=4)


def contribute(prior, sensitivity, pattern, ownership, obs_dev):
    members_dev = prior.shape[0]
    blocks, slots, obs_block, params = sensitivity.shape
    tiles = lax.axis_size("tile")
    owned = obs_dev // obs_block
    lanes = 128
    groups = owned // (lanes // members_dev)
    half = jax.ShapeDtypeStruct((tiles, groups * obs_block, lanes), jnp.float32)
    hbm = pl.BlockSpec(memory_space=pl.ANY)
    return pl.pallas_call(
        functools.partial(contribute_kernel, owned, min(3, blocks)),
        in_specs=[SMEM, SMEM, hbm, hbm],
        out_specs=[VMEM, VMEM, VMEM],
        out_shape=[half, half, jax.ShapeDtypeStruct(prior.shape, jnp.bfloat16)],
        scratch_shapes=[
            pltpu.VMEM((blocks, slots * obs_block, params), jnp.bfloat16),
            pltpu.VMEM(prior.shape, jnp.float32),
            pltpu.VMEM((2 * tiles * groups, obs_block, lanes), jnp.float32),
            pltpu.SMEM(ownership.shape, jnp.int32),
            pltpu.SemaphoreType.DMA((blocks,)),
            pltpu.SemaphoreType.DMA((blocks,)),
        ],
        name="contribute",
    )(pattern, ownership, prior, sensitivity.reshape(blocks, slots * obs_block, params))


def gram_kernel(count, *refs):
    predicted, noise = refs[:count], refs[count : 2 * count]
    observed, sigma, keep, send, stack, whole = refs[2 * count :]
    members_dev = noise[0].shape[0]
    members = members_dev * count
    width, lanes = predicted[0].shape
    at = lax.axis_index("member")
    for r in range(count):
        rows = pl.ds(pl.multiple_of((at ^ r) * members_dev, members_dev), members_dev)
        turned = predicted[r][...].T
        for q in range(lanes // members_dev):
            stack[rows, q * width : (q + 1) * width] = turned[
                q * members_dev : (q + 1) * members_dev
            ]
        whole_rows = pl.ds(pl.multiple_of(members + (at ^ r) * members_dev, members_dev), members_dev)
        stack[whole_rows, :] = noise[r][...]
    values = stack[:members, :]
    inverse = 1.0 / sigma[...]
    spread = (values - jnp.mean(values, axis=0, keepdims=True)) * (
        inverse * (1.0 / math.sqrt(members - 1))
    )
    innovation = (observed[...] - values) * inverse + stack[members:, :]
    stack[:members, :] = spread
    stack[members:, :] = innovation
    misfit = jnp.sum(jnp.sum(innovation * innovation, axis=0, keepdims=True), axis=1, keepdims=True)
    both = lax.dot_general(
        spread, stack[...], NT, precision=EXACT, preferred_element_type=jnp.float32
    )
    row = lax.broadcasted_iota(jnp.int32, both.shape, 0)
    col = lax.broadcasted_iota(jnp.int32, both.shape, 1)
    whole[...] = both + jnp.where(row == col, misfit * (1.0 / (4.0 * members * members)), 0.0)
    rows = members // 2
    side = lax.axis_index("slab")
    keep[...] = whole[pl.ds(pl.multiple_of(side * rows, rows), rows), :]
    send[...] = whole[pl.ds(pl.multiple_of((1 - side) * rows, rows), rows), :]


def gram(predicted, noise, observed, sigma):
    count = len(predicted)
    members_dev, obs_dev = noise[0].shape
    members = members_dev * count
    half = jax.ShapeDtypeStruct((members // 2, 2 * members), jnp.float32)
    return pl.pallas_call(
        functools.partial(gram_kernel, count),
        in_specs=[VMEM] * (2 * count + 2),
        out_specs=[VMEM, VMEM],
        out_shape=[half, half],
        scratch_shapes=[
            pltpu.VMEM((2 * members, obs_dev), jnp.float32),
            pltpu.VMEM((members, 2 * members), jnp.float32),
        ],
        compiler_params=pltpu.CompilerParams(vmem_limit_bytes=8 << 20),
        name="gram",
    )(*predicted, *noise, observed.reshape(1, obs_dev), sigma.reshape(1, obs_dev))


def update_kernel(count, *refs):
    mine, other = refs[:2]
    prior = refs[2 : 2 + count]
    increment, weights, both, cols, ensemble, sems = refs[2 + count :]
    members = weights.shape[0]
    members_dev = members // count
    at = lax.axis_index("member")
    side = lax.axis_index("slab")
    copies = []
    for r in range(count):
        rows = pl.ds(pl.multiple_of((at ^ r) * members_dev, members_dev), members_dev)
        copies.append(pltpu.make_async_copy(prior[r], ensemble.at[rows, :], sems.at[r]))
        copies[-1].start()
    half = members // 2
    both[pl.ds(pl.multiple_of(side * half, half), half), :] = mine[...]
    both[pl.ds(pl.multiple_of((1 - side) * half, half), half), :] = other[...]
    row = lax.broadcasted_iota(jnp.int32, (members, members), 0)
    col = lax.broadcasted_iota(jnp.int32, (members, members), 1)
    eye = jnp.where(row == col, 1.0, 0.0)
    system = both[:, :members]

    def total(x):
        return jnp.sum(jnp.sum(x, axis=0, keepdims=True), axis=1, keepdims=True)

    trace = total(system * eye)
    system = system + trace * (1.0 / (members * members))
    bound = jnp.max(jnp.sum(jnp.abs(system), axis=0, keepdims=True), axis=1, keepdims=True)
    scale = jnp.minimum(trace * (1.0 + 1.0 / members) / total(system * system), 1.9 / bound)
    power = eye - scale * system
    terms = both[:, members:] * scale

    def step(power, terms):
        pair = lax.dot_general(
            power,
            jnp.concatenate([power, terms], axis=1),
            (((1,), (0,)), ((), ())),
            precision=EXACT,
            preferred_element_type=jnp.float32,
        )
        return pair[:, :members], terms + pair[:, members:]

    for _ in range(5):
        power, terms = step(power, terms)

    def unfinished(carry):
        power, _, count = carry
        return (jnp.sum(power * power) > 1e-12) & (count < 40)

    def further(carry):
        power, terms, count = carry
        power, terms = step(power, terms)
        return power, terms, count + 1

    _, terms, _ = lax.while_loop(unfinished, further, (power, terms, 0))
    weights[...] = terms
    centred = (terms - jnp.mean(terms, axis=0, keepdims=True)) * (1.0 / math.sqrt(members - 1))
    cols[...] = centred.T
    own = cols[pl.ds(pl.multiple_of(at * members_dev, members_dev), members_dev), :].astype(
        jnp.bfloat16
    )
    for copy in copies:
        copy.wait()
    width = 512

    def multiply(n, carry):
        lanes = pl.ds(pl.multiple_of(n * width, width), width)
        increment[:, lanes] = jnp.dot(own, ensemble[:, lanes], preferred_element_type=jnp.float32)
        return carry

    lax.fori_loop(0, increment.shape[1] // width, multiply, 0, unroll=True)


def update(mine, other, prior):
    count = len(prior)
    members_dev, params = prior[0].shape
    members = members_dev * count
    return pl.pallas_call(
        functools.partial(update_kernel, count),
        in_specs=[VMEM, VMEM] + [pl.BlockSpec(memory_space=pl.ANY)] * count,
        out_specs=[VMEM, VMEM],
        out_shape=[
            jax.ShapeDtypeStruct((members_dev, params), jnp.float32),
            jax.ShapeDtypeStruct((members, members), jnp.float32),
        ],
        scratch_shapes=[
            pltpu.VMEM((members, 2 * members), jnp.float32),
            pltpu.VMEM((members, members), jnp.float32),
            pltpu.VMEM((members, params), jnp.bfloat16),
            pltpu.SemaphoreType.DMA((count,)),
        ],
        compiler_params=pltpu.CompilerParams(vmem_limit_bytes=8 << 20),
        name="update",
    )(mine, other, *prior)


def step(prior, sensitivity, pattern, ownership, observed, obs_noise, perturbation):
    obs_dev = observed.shape[0]
    tiles = lax.axis_size("tile")
    keep, send, prior_bf = contribute(prior, sensitivity, pattern, ownership, obs_dev)
    got = swap(send, "slab", 1)
    chunks = [keep[r] + got[r] for r in range(tiles)]
    chunks, perturbation = lax.optimization_barrier((chunks, perturbation))
    noise = gather_xor(perturbation, "member")
    ensemble = gather_xor(prior_bf, "member")
    for shift, radix in digits(tiles):
        low = 1 << shift
        arrived = [
            [swap(chunks[d * low + r], "tile", d << shift) for r in range(low)]
            for d in range(1, radix)
        ]
        chunks = [sum((g[r] for g in arrived), chunks[r]) for r in range(low)]
    predicted = gather_xor(chunks[0], "member")
    keep, send = gram(predicted, noise, observed, obs_noise)
    mine = keep + swap(send, "slab", 1)
    for shift, radix in digits(tiles)[::-1]:
        mine = sum((swap(mine, "tile", d << shift) for d in range(1, radix)), mine)
    return tuple(update(mine, swap(mine, "slab", 1), ensemble))


def solution(mesh):
    return jax.shard_map(
        step,
        mesh=mesh,
        in_specs=(
            P("member", ("slab", "tile")),
            P(("slab", "tile"), None, None, None),
            P(("slab", "tile"), None),
            P(),
            P(("slab", "tile")),
            P(("slab", "tile")),
            P("member", ("slab", "tile")),
        ),
        out_specs=(P("member", ("slab", "tile")), P()),
        check_vma=False,
    )
```

```python
import functools
import math

import jax
import jax.numpy as jnp
from jax import lax
from jax.experimental import pallas as pl
from jax.experimental.pallas import tpu as pltpu
from jax.sharding import PartitionSpec as P


EXACT = lax.Precision.HIGHEST
VMEM = pl.BlockSpec(memory_space=pltpu.VMEM)
SMEM = pl.BlockSpec(memory_space=pltpu.SMEM)
NT = (((1,), (1,)), ((), ()))


def swap(x, axis, distance):
    size = lax.axis_size(axis)
    return lax.ppermute(x, axis, [(i, i ^ distance) for i in range(size)])


def digits(size):
    out, shift = [], 0
    while size > 1:
        radix = 4 if size % 4 == 0 else 2
        out.append((shift, radix))
        shift += radix.bit_length() - 1
        size //= radix
    return out[::-1]


def gather_xor(x, axis):
    return [x] + [swap(x, axis, r) for r in range(1, lax.axis_size(axis))]


def contribute_kernel(
    owned,
    depth,
    pattern_ref,
    ownership_ref,
    prior_hbm,
    sens_hbm,
    keep_ref,
    send_ref,
    bf_ref,
    sens,
    prior,
    acc,
    storage,
    sens_sems,
    prior_sems,
):
    blocks, slots = pattern_ref.shape
    tiles, _, lanes = keep_ref.shape
    members_dev = prior.shape[0]
    _, rows_block, params = sens.shape
    obs_block = rows_block // slots
    copies = lanes // members_dev
    groups = owned // copies
    me = lax.axis_index("slab") * tiles + lax.axis_index("tile")

    def cols(b):
        return pl.ds(pl.multiple_of(b * params, params), params)

    def fetch(b):
        return (
            pltpu.make_async_copy(prior_hbm.at[:, cols(b)], prior.at[:, cols(b)], prior_sems.at[b]),
            pltpu.make_async_copy(sens_hbm.at[b], sens.at[b], sens_sems.at[b]),
        )

    for b in range(depth):
        for copy in fetch(b):
            copy.start()

    def place(s, carry):
        storage[ownership_ref[s]] = s ^ (me * owned)
        return carry

    lax.fori_loop(0, ownership_ref.shape[0], place, 0, unroll=8)
    acc[...] = jnp.zeros_like(acc)
    lane_group = lax.broadcasted_iota(jnp.int32, (obs_block, lanes), 1) // members_dev

    def work(b, carry):
        @pl.when(b + depth < blocks)
        def _():
            for copy in fetch(b + depth):
                copy.start()

        for copy in fetch(b):
            copy.wait()
        rows = prior[:, cols(b)].astype(jnp.bfloat16)
        bf_ref[:, cols(b)] = rows
        rows = jnp.concatenate([rows] * copies, axis=0)

        def add(count):
            terms = lax.dot_general(
                sens[b, : count * obs_block], rows, NT, preferred_element_type=jnp.float32
            )
            for k in range(count):
                block = pattern_ref[b, k]
                at = storage[jnp.maximum(block, 0)]
                group = jnp.where(block >= 0, (at % owned) // groups, -1)
                acc[(at // owned) * groups + at % groups] += jnp.where(
                    lane_group == group, terms[k * obs_block : (k + 1) * obs_block], 0.0
                )

        counts = list(range(slots // 4, slots + 1, 4))
        for low, count in zip([0] + counts[:-1], counts):
            fits = (low == 0) | (pattern_ref[b, low] >= 0)
            if count < slots:
                fits = fits & (pattern_ref[b, count] < 0)
            pl.when(fits)(functools.partial(add, count))
        return carry

    lax.fori_loop(0, blocks, work, 0)

    def flush(r, carry):
        for g in range(groups):
            rows = slice(g * obs_block, (g + 1) * obs_block)
            keep_ref[r, rows, :] = acc[r * groups + g]
            send_ref[r, rows, :] = acc[(tiles + r) * groups + g]
        return carry

    lax.fori_loop(0, tiles, flush, 0, unroll=4)


def contribute(prior, sensitivity, pattern, ownership, obs_dev):
    members_dev = prior.shape[0]
    blocks, slots, obs_block, params = sensitivity.shape
    tiles = lax.axis_size("tile")
    owned = obs_dev // obs_block
    lanes = 128
    groups = owned // (lanes // members_dev)
    half = jax.ShapeDtypeStruct((tiles, groups * obs_block, lanes), jnp.float32)
    hbm = pl.BlockSpec(memory_space=pl.ANY)
    return pl.pallas_call(
        functools.partial(contribute_kernel, owned, min(3, blocks)),
        in_specs=[SMEM, SMEM, hbm, hbm],
        out_specs=[VMEM, VMEM, VMEM],
        out_shape=[half, half, jax.ShapeDtypeStruct(prior.shape, jnp.bfloat16)],
        scratch_shapes=[
            pltpu.VMEM((blocks, slots * obs_block, params), jnp.bfloat16),
            pltpu.VMEM(prior.shape, jnp.float32),
            pltpu.VMEM((2 * tiles * groups, obs_block, lanes), jnp.float32),
            pltpu.SMEM(ownership.shape, jnp.int32),
            pltpu.SemaphoreType.DMA((blocks,)),
            pltpu.SemaphoreType.DMA((blocks,)),
        ],
        name="contribute",
    )(pattern, ownership, prior, sensitivity.reshape(blocks, slots * obs_block, params))


def gram_kernel(count, *refs):
    predicted, noise = refs[:count], refs[count : 2 * count]
    observed, sigma, keep, send, stack, whole = refs[2 * count :]
    members_dev = noise[0].shape[0]
    members = members_dev * count
    width, lanes = predicted[0].shape
    at = lax.axis_index("member")
    for r in range(count):
        rows = pl.ds(pl.multiple_of((at ^ r) * members_dev, members_dev), members_dev)
        turned = predicted[r][...].T
        for q in range(lanes // members_dev):
            stack[rows, q * width : (q + 1) * width] = turned[
                q * members_dev : (q + 1) * members_dev
            ]
        whole_rows = pl.ds(pl.multiple_of(members + (at ^ r) * members_dev, members_dev), members_dev)
        stack[whole_rows, :] = noise[r][...]
    values = stack[:members, :]
    inverse = 1.0 / sigma[...]
    spread = (values - jnp.mean(values, axis=0, keepdims=True)) * (
        inverse * (1.0 / math.sqrt(members - 1))
    )
    innovation = (observed[...] - values) * inverse + stack[members:, :]
    stack[:members, :] = spread
    stack[members:, :] = innovation
    misfit = jnp.sum(jnp.sum(innovation * innovation, axis=0, keepdims=True), axis=1, keepdims=True)
    both = lax.dot_general(
        spread, stack[...], NT, precision=EXACT, preferred_element_type=jnp.float32
    )
    row = lax.broadcasted_iota(jnp.int32, both.shape, 0)
    col = lax.broadcasted_iota(jnp.int32, both.shape, 1)
    whole[...] = both + jnp.where(row == col, misfit * (1.0 / (4.0 * members * members)), 0.0)
    rows = members // 2
    side = lax.axis_index("slab")
    keep[...] = whole[pl.ds(pl.multiple_of(side * rows, rows), rows), :]
    send[...] = whole[pl.ds(pl.multiple_of((1 - side) * rows, rows), rows), :]


def gram(predicted, noise, observed, sigma):
    count = len(predicted)
    members_dev, obs_dev = noise[0].shape
    members = members_dev * count
    half = jax.ShapeDtypeStruct((members // 2, 2 * members), jnp.float32)
    return pl.pallas_call(
        functools.partial(gram_kernel, count),
        in_specs=[VMEM] * (2 * count + 2),
        out_specs=[VMEM, VMEM],
        out_shape=[half, half],
        scratch_shapes=[
            pltpu.VMEM((2 * members, obs_dev), jnp.float32),
            pltpu.VMEM((members, 2 * members), jnp.float32),
        ],
        compiler_params=pltpu.CompilerParams(vmem_limit_bytes=8 << 20),
        name="gram",
    )(*predicted, *noise, observed.reshape(1, obs_dev), sigma.reshape(1, obs_dev))


def update_kernel(count, *refs):
    mine, other = refs[:2]
    prior = refs[2 : 2 + count]
    increment, weights, both, cols, ensemble, result, sems, out_sems = refs[2 + count :]
    members = weights.shape[0]
    members_dev = members // count
    at = lax.axis_index("member")
    side = lax.axis_index("slab")
    copies = []
    for r in range(1, count):
        rows = pl.ds(pl.multiple_of((at ^ r) * members_dev, members_dev), members_dev)
        copies.append(pltpu.make_async_copy(prior[r], ensemble.at[rows, :], sems.at[r]))
        copies[-1].start()
    own_rows = pl.ds(pl.multiple_of(at * members_dev, members_dev), members_dev)
    ensemble[own_rows, :] = prior[0][...].astype(jnp.bfloat16)
    half = members // 2
    both[pl.ds(pl.multiple_of(side * half, half), half), :] = mine[...]
    both[pl.ds(pl.multiple_of((1 - side) * half, half), half), :] = other[...]
    row = lax.broadcasted_iota(jnp.int32, (members, members), 0)
    col = lax.broadcasted_iota(jnp.int32, (members, members), 1)
    eye = jnp.where(row == col, 1.0, 0.0)
    system = both[:, :members]

    def total(x):
        return jnp.sum(jnp.sum(x, axis=0, keepdims=True), axis=1, keepdims=True)

    trace = total(system * eye)
    system = system + trace * (1.0 / (members * members))
    bound = jnp.max(jnp.sum(jnp.abs(system), axis=0, keepdims=True), axis=1, keepdims=True)
    scale = jnp.minimum(trace * (1.0 + 1.0 / members) / total(system * system), 1.9 / bound)
    power = eye - scale * system
    terms = both[:, members:] * scale

    def step(power, terms):
        pair = lax.dot_general(
            power,
            jnp.concatenate([power, terms], axis=1),
            (((1,), (0,)), ((), ())),
            precision=EXACT,
            preferred_element_type=jnp.float32,
        )
        return pair[:, :members], terms + pair[:, members:]

    for _ in range(5):
        power, terms = step(power, terms)

    def unfinished(carry):
        power, _, count = carry
        return (jnp.sum(power * power) > 1e-12) & (count < 40)

    def further(carry):
        power, terms, count = carry
        power, terms = step(power, terms)
        return power, terms, count + 1

    _, terms, _ = lax.while_loop(unfinished, further, (power, terms, 0))
    weights[...] = terms
    centred = (terms - jnp.mean(terms, axis=0, keepdims=True)) * (1.0 / math.sqrt(members - 1))
    cols[...] = centred.T
    own = cols[own_rows, :].astype(jnp.bfloat16)
    for copy in copies:
        copy.wait()
    outs = []
    width = result.shape[1] // out_sems.shape[0]
    for n in range(out_sems.shape[0]):
        lanes = pl.ds(n * width, width)
        result[:, lanes] = jnp.dot(own, ensemble[:, lanes], preferred_element_type=jnp.float32)
        outs.append(
            pltpu.make_async_copy(result.at[:, lanes], increment.at[:, lanes], out_sems.at[n])
        )
        outs[-1].start()
    for copy in outs:
        copy.wait()


def update(mine, other, prior):
    count = len(prior)
    members_dev, params = prior[0].shape
    members = members_dev * count
    return pl.pallas_call(
        functools.partial(update_kernel, count),
        in_specs=[VMEM, VMEM, VMEM] + [pl.BlockSpec(memory_space=pl.ANY)] * (count - 1),
        out_specs=[pl.BlockSpec(memory_space=pl.ANY), VMEM],
        out_shape=[
            jax.ShapeDtypeStruct((members_dev, params), jnp.float32),
            jax.ShapeDtypeStruct((members, members), jnp.float32),
        ],
        scratch_shapes=[
            pltpu.VMEM((members, 2 * members), jnp.float32),
            pltpu.VMEM((members, members), jnp.float32),
            pltpu.VMEM((members, params), jnp.bfloat16),
            pltpu.VMEM((members_dev, params), jnp.float32),
            pltpu.SemaphoreType.DMA((count,)),
            pltpu.SemaphoreType.DMA((4,)),
        ],
        compiler_params=pltpu.CompilerParams(vmem_limit_bytes=8 << 20),
        name="update",
    )(mine, other, *prior)


def step(prior, sensitivity, pattern, ownership, observed, obs_noise, perturbation):
    obs_dev = observed.shape[0]
    tiles = lax.axis_size("tile")
    keep, send, prior_bf = contribute(prior, sensitivity, pattern, ownership, obs_dev)
    got = swap(send, "slab", 1)
    chunks = [keep[r] + got[r] for r in range(tiles)]
    chunks, perturbation = lax.optimization_barrier((chunks, perturbation))
    noise = gather_xor(perturbation, "member")
    ensemble = [prior] + gather_xor(prior_bf, "member")[1:]
    for shift, radix in digits(tiles):
        low = 1 << shift
        arrived = [
            [swap(chunks[d * low + r], "tile", d << shift) for r in range(low)]
            for d in range(1, radix)
        ]
        chunks = [sum((g[r] for g in arrived), chunks[r]) for r in range(low)]
    predicted = gather_xor(chunks[0], "member")
    keep, send = gram(predicted, noise, observed, obs_noise)
    mine = keep + swap(send, "slab", 1)
    for shift, radix in digits(tiles)[::-1]:
        mine = sum((swap(mine, "tile", d << shift) for d in range(1, radix)), mine)
    return tuple(update(mine, swap(mine, "slab", 1), ensemble))


def solution(mesh):
    return jax.shard_map(
        step,
        mesh=mesh,
        in_specs=(
            P("member", ("slab", "tile")),
            P(("slab", "tile"), None, None, None),
            P(("slab", "tile"), None),
            P(),
            P(("slab", "tile")),
            P(("slab", "tile")),
            P("member", ("slab", "tile")),
        ),
        out_specs=(P("member", ("slab", "tile")), P()),
        check_vma=False,
    )
```

```python
import functools
import math

import jax
import jax.numpy as jnp
from jax import lax
from jax.experimental import pallas as pl
from jax.experimental.pallas import tpu as pltpu
from jax.sharding import PartitionSpec as P


EXACT = lax.Precision.HIGHEST
VMEM = pl.BlockSpec(memory_space=pltpu.VMEM)
SMEM = pl.BlockSpec(memory_space=pltpu.SMEM)
NT = (((1,), (1,)), ((), ()))


def swap(x, axis, distance):
    size = lax.axis_size(axis)
    return lax.ppermute(x, axis, [(i, i ^ distance) for i in range(size)])


def digits(size):
    out, shift = [], 0
    while size > 1:
        radix = 4 if size % 4 == 0 else 2
        out.append((shift, radix))
        shift += radix.bit_length() - 1
        size //= radix
    return out[::-1]


def gather_xor(x, axis):
    return [x] + [swap(x, axis, r) for r in range(1, lax.axis_size(axis))]


def contribute_kernel(
    owned,
    depth,
    pattern_ref,
    ownership_ref,
    prior_hbm,
    sens_hbm,
    keep_ref,
    send_ref,
    bf_ref,
    sens,
    prior,
    acc,
    storage,
    sens_sems,
    prior_sems,
):
    blocks, slots = pattern_ref.shape
    tiles, _, lanes = keep_ref.shape
    members_dev = prior.shape[0]
    _, rows_block, params = sens.shape
    obs_block = rows_block // slots
    copies = lanes // members_dev
    groups = owned // copies
    me = lax.axis_index("slab") * tiles + lax.axis_index("tile")

    def cols(b):
        return pl.ds(pl.multiple_of(b * params, params), params)

    def fetch(b):
        return (
            pltpu.make_async_copy(prior_hbm.at[:, cols(b)], prior.at[:, cols(b)], prior_sems.at[b]),
            pltpu.make_async_copy(sens_hbm.at[b], sens.at[b], sens_sems.at[b]),
        )

    for b in range(depth):
        for copy in fetch(b):
            copy.start()

    def place(s, carry):
        storage[ownership_ref[s]] = s ^ (me * owned)
        return carry

    lax.fori_loop(0, ownership_ref.shape[0], place, 0, unroll=8)
    acc[...] = jnp.zeros_like(acc)
    lane_group = lax.broadcasted_iota(jnp.int32, (obs_block, lanes), 1) // members_dev

    def work(b, carry):
        @pl.when(b + depth < blocks)
        def _():
            for copy in fetch(b + depth):
                copy.start()

        for copy in fetch(b):
            copy.wait()
        rows = prior[:, cols(b)].astype(jnp.bfloat16)
        bf_ref[:, cols(b)] = rows
        rows = jnp.concatenate([rows] * copies, axis=0)

        def add(count):
            terms = lax.dot_general(
                sens[b, : count * obs_block], rows, NT, preferred_element_type=jnp.float32
            )
            for k in range(count):
                block = pattern_ref[b, k]
                at = storage[jnp.maximum(block, 0)]
                group = jnp.where(block >= 0, (at % owned) // groups, -1)
                acc[(at // owned) * groups + at % groups] += jnp.where(
                    lane_group == group, terms[k * obs_block : (k + 1) * obs_block], 0.0
                )

        counts = list(range(slots // 4, slots + 1, 4))
        for low, count in zip([0] + counts[:-1], counts):
            fits = (low == 0) | (pattern_ref[b, low] >= 0)
            if count < slots:
                fits = fits & (pattern_ref[b, count] < 0)
            pl.when(fits)(functools.partial(add, count))
        return carry

    lax.fori_loop(0, blocks, work, 0)

    def flush(r, carry):
        for g in range(groups):
            rows = slice(g * obs_block, (g + 1) * obs_block)
            keep_ref[r, rows, :] = acc[r * groups + g]
            send_ref[r, rows, :] = acc[(tiles + r) * groups + g]
        return carry

    lax.fori_loop(0, tiles, flush, 0, unroll=4)


def contribute(prior, sensitivity, pattern, ownership, obs_dev):
    members_dev = prior.shape[0]
    blocks, slots, obs_block, params = sensitivity.shape
    tiles = lax.axis_size("tile")
    owned = obs_dev // obs_block
    lanes = 128
    groups = owned // (lanes // members_dev)
    half = jax.ShapeDtypeStruct((tiles, groups * obs_block, lanes), jnp.float32)
    hbm = pl.BlockSpec(memory_space=pl.ANY)
    return pl.pallas_call(
        functools.partial(contribute_kernel, owned, min(3, blocks)),
        in_specs=[SMEM, SMEM, hbm, hbm],
        out_specs=[VMEM, VMEM, VMEM],
        out_shape=[half, half, jax.ShapeDtypeStruct(prior.shape, jnp.bfloat16)],
        scratch_shapes=[
            pltpu.VMEM((blocks, slots * obs_block, params), jnp.bfloat16),
            pltpu.VMEM(prior.shape, jnp.float32),
            pltpu.VMEM((2 * tiles * groups, obs_block, lanes), jnp.float32),
            pltpu.SMEM(ownership.shape, jnp.int32),
            pltpu.SemaphoreType.DMA((blocks,)),
            pltpu.SemaphoreType.DMA((blocks,)),
        ],
        name="contribute",
    )(pattern, ownership, prior, sensitivity.reshape(blocks, slots * obs_block, params))


def gram_kernel(count, *refs):
    predicted, noise = refs[:count], refs[count : 2 * count]
    observed, sigma, keep, send, stack, whole = refs[2 * count :]
    members_dev = noise[0].shape[0]
    members = members_dev * count
    width, lanes = predicted[0].shape
    at = lax.axis_index("member")
    for r in range(count):
        rows = pl.ds(pl.multiple_of((at ^ r) * members_dev, members_dev), members_dev)
        turned = predicted[r][...].T
        for q in range(lanes // members_dev):
            stack[rows, q * width : (q + 1) * width] = turned[
                q * members_dev : (q + 1) * members_dev
            ]
        whole_rows = pl.ds(pl.multiple_of(members + (at ^ r) * members_dev, members_dev), members_dev)
        stack[whole_rows, :] = noise[r][...]
    values = stack[:members, :]
    inverse = 1.0 / sigma[...]
    spread = (values - jnp.mean(values, axis=0, keepdims=True)) * (
        inverse * (1.0 / math.sqrt(members - 1))
    )
    innovation = (observed[...] - values) * inverse + stack[members:, :]
    stack[:members, :] = spread
    stack[members:, :] = innovation
    misfit = jnp.sum(jnp.sum(innovation * innovation, axis=0, keepdims=True), axis=1, keepdims=True)
    both = lax.dot_general(
        spread, stack[...], NT, precision=EXACT, preferred_element_type=jnp.float32
    )
    row = lax.broadcasted_iota(jnp.int32, both.shape, 0)
    col = lax.broadcasted_iota(jnp.int32, both.shape, 1)
    both = both + jnp.where(row == col, misfit * (1.0 / (4.0 * members * members)), 0.0)
    system, cross = both[:, :members], both[:, members:]
    half = members // 2
    first, last = system[:half, :half], system[half:, half:]
    above = row[:half, :half] <= col[:half, :half]
    whole[: members, :] = cross
    whole[members : members + half, :half] = system[:half, half:]
    whole[members : members + half, half:] = jnp.where(above, first, last)
    diagonal = jnp.sum(jnp.where(row == col, both, 0.0)[:, :members], axis=0, keepdims=True)
    side = lax.axis_index("slab")
    for out, at in ((keep, side), (send, 1 - side)):
        out[:half, :] = whole[pl.ds(pl.multiple_of(at * half, half), half), :]
        quarter = half // 2
        out[half : half + quarter, :] = whole[
            pl.ds(pl.multiple_of(members + at * quarter, quarter), quarter), :
        ]
        out[half + quarter :, :] = jnp.broadcast_to(diagonal, (8, members))


def gram(predicted, noise, observed, sigma):
    count = len(predicted)
    members_dev, obs_dev = noise[0].shape
    members = members_dev * count
    half = jax.ShapeDtypeStruct((members // 2 + members // 4 + 8, members), jnp.float32)
    return pl.pallas_call(
        functools.partial(gram_kernel, count),
        in_specs=[VMEM] * (2 * count + 2),
        out_specs=[VMEM, VMEM],
        out_shape=[half, half],
        scratch_shapes=[
            pltpu.VMEM((2 * members, obs_dev), jnp.float32),
            pltpu.VMEM((members + members // 2, members), jnp.float32),
        ],
        compiler_params=pltpu.CompilerParams(vmem_limit_bytes=8 << 20),
        name="gram",
    )(*predicted, *noise, observed.reshape(1, obs_dev), sigma.reshape(1, obs_dev))


def update_kernel(count, *refs):
    mine, other = refs[:2]
    prior = refs[2 : 2 + count]
    increment, weights, cross, packed, cols, ensemble, _, _ = refs[2 + count :]
    members = weights.shape[0]
    members_dev = members // count
    at = lax.axis_index("member")
    side = lax.axis_index("slab")
    own_rows = pl.ds(pl.multiple_of(at * members_dev, members_dev), members_dev)
    for r in range(count):
        rows = pl.ds(pl.multiple_of((at ^ r) * members_dev, members_dev), members_dev)
        ensemble[rows, :] = prior[r][...].astype(jnp.bfloat16)
    half, quarter = members // 2, members // 4
    for part, at_side in ((mine, side), (other, 1 - side)):
        cross[pl.ds(pl.multiple_of(at_side * half, half), half), :] = part[:half, :]
        packed[pl.ds(pl.multiple_of(at_side * quarter, quarter), quarter), :] = part[
            half : half + quarter, :
        ]
    row = lax.broadcasted_iota(jnp.int32, (members, members), 0)
    col = lax.broadcasted_iota(jnp.int32, (members, members), 1)
    eye = jnp.where(row == col, 1.0, 0.0)
    top = packed[...]
    turned = top.T
    mixed, mixed_turned = top[:, half:], turned[half:, :]
    above = row[:half, :half] <= col[:half, :half]
    system = jnp.concatenate(
        [
            jnp.concatenate([jnp.where(above, mixed, mixed_turned), top[:, :half]], axis=1),
            jnp.concatenate([turned[:half, :], jnp.where(above, mixed_turned, mixed)], axis=1),
        ],
        axis=0,
    )
    system = jnp.where(row == col, mine[half + quarter : half + quarter + 1, :], system)

    def total(x):
        return jnp.sum(jnp.sum(x, axis=0, keepdims=True), axis=1, keepdims=True)

    trace = total(system * eye)
    system = system + (trace - total(system)) * (1.0 / (members * members))
    bound = jnp.max(jnp.sum(jnp.abs(system), axis=0, keepdims=True), axis=1, keepdims=True)

    def begin(scale):
        return eye - scale * system, cross[...] * scale

    power, terms = begin(total(system * eye) / total(system * system))

    def step(power, terms):
        pair = lax.dot_general(
            power,
            jnp.concatenate([power, terms], axis=1),
            (((1,), (0,)), ((), ())),
            precision=EXACT,
            preferred_element_type=jnp.float32,
        )
        return pair[:, :members], terms + pair[:, members:]

    for _ in range(4):
        power, terms = step(power, terms)

    def unfinished(carry):
        power, _, count = carry
        return (jnp.sum(power * power) > 1e-12) & (count < 40)

    def further(carry):
        power, terms, count = carry
        power, terms = step(power, terms)
        return power, terms, count + 1

    shrinks = jnp.sum(power * power, axis=0, keepdims=True)
    shrinks = jnp.sum(shrinks, axis=1, keepdims=True) < 1.0
    sure_power, sure_terms = begin(1.9 / bound)
    power = jnp.where(shrinks, power, sure_power)
    terms = jnp.where(shrinks, terms, sure_terms)
    _, terms, _ = lax.while_loop(unfinished, further, (power, terms, 0))
    weights[...] = terms
    centred = (terms - jnp.mean(terms, axis=0, keepdims=True)) * (1.0 / math.sqrt(members - 1))
    cols[...] = centred.T
    own = cols[own_rows, :].astype(jnp.bfloat16)
    for n in range(4):
        lanes = pl.ds(n * 1024, 1024)
        increment[:, lanes] = jnp.dot(own, ensemble[:, lanes], preferred_element_type=jnp.float32)


def update(mine, other, prior):
    count = len(prior)
    members_dev, params = prior[0].shape
    members = members_dev * count
    return pl.pallas_call(
        functools.partial(update_kernel, count),
        in_specs=[VMEM] * (2 + count),
        out_specs=[VMEM, VMEM],
        out_shape=[
            jax.ShapeDtypeStruct((members_dev, params), jnp.float32),
            jax.ShapeDtypeStruct((members, members), jnp.float32),
        ],
        scratch_shapes=[
            pltpu.VMEM((members, members), jnp.float32),
            pltpu.VMEM((members // 2, members), jnp.float32),
            pltpu.VMEM((members, members), jnp.float32),
            pltpu.VMEM((members, params), jnp.bfloat16),
            pltpu.VMEM((members_dev, params), jnp.float32),
            pltpu.SemaphoreType.DMA((4,)),
        ],
        compiler_params=pltpu.CompilerParams(vmem_limit_bytes=8 << 20),
        name="update",
    )(mine, other, *prior)


def step(prior, sensitivity, pattern, ownership, observed, obs_noise, perturbation):
    obs_dev = observed.shape[0]
    tiles = lax.axis_size("tile")
    keep, send, prior_bf = contribute(prior, sensitivity, pattern, ownership, obs_dev)
    got = swap(send, "slab", 1)
    chunks = [keep[r] + got[r] for r in range(tiles)]
    chunks, perturbation = lax.optimization_barrier((chunks, perturbation))
    noise = gather_xor(perturbation, "member")
    ensemble = [prior] + gather_xor(prior_bf, "member")[1:]
    for shift, radix in digits(tiles):
        low = 1 << shift
        arrived = [
            [swap(chunks[d * low + r], "tile", d << shift) for r in range(low)]
            for d in range(1, radix)
        ]
        chunks = [sum((g[r] for g in arrived), chunks[r]) for r in range(low)]
    predicted = gather_xor(chunks[0], "member")
    keep, send = gram(predicted, noise, observed, obs_noise)
    mine = keep + swap(send, "slab", 1)
    for shift, radix in digits(tiles)[::-1]:
        mine = sum((swap(mine, "tile", d << shift) for d in range(1, radix)), mine)
    return tuple(update(mine, swap(mine, "slab", 1), ensemble))


def solution(mesh):
    return jax.shard_map(
        step,
        mesh=mesh,
        in_specs=(
            P("member", ("slab", "tile")),
            P(("slab", "tile"), None, None, None),
            P(("slab", "tile"), None),
            P(),
            P(("slab", "tile")),
            P(("slab", "tile")),
            P("member", ("slab", "tile")),
        ),
        out_specs=(P("member", ("slab", "tile")), P()),
        check_vma=False,
    )
```

```python
import functools
import math

import jax
import jax.numpy as jnp
from jax import lax
from jax.experimental import pallas as pl
from jax.experimental.pallas import tpu as pltpu
from jax.sharding import PartitionSpec as P


EXACT = lax.Precision.HIGHEST
VMEM = pl.BlockSpec(memory_space=pltpu.VMEM)
SMEM = pl.BlockSpec(memory_space=pltpu.SMEM)
NT = (((1,), (1,)), ((), ()))


def swap(x, axis, distance):
    size = lax.axis_size(axis)
    return lax.ppermute(x, axis, [(i, i ^ distance) for i in range(size)])


def digits(size):
    out, shift = [], 0
    while size > 1:
        radix = 4 if size % 4 == 0 else 2
        out.append((shift, radix))
        shift += radix.bit_length() - 1
        size //= radix
    return out[::-1]


def gather_xor(x, axis):
    return [x] + [swap(x, axis, r) for r in range(1, lax.axis_size(axis))]


def contribute_kernel(
    owned,
    depth,
    slots,
    table,
    prior_hbm,
    sens_hbm,
    keep_ref,
    send_ref,
    bf_ref,
    sens,
    prior,
    acc,
    storage,
    sens_sems,
    prior_sems,
):
    blocks = sens.shape[0]
    tiles, _, lanes = keep_ref.shape
    members_dev = prior.shape[0]
    _, rows_block, params = sens.shape
    obs_block = rows_block // slots
    copies = lanes // members_dev
    groups = owned // copies
    me = lax.axis_index("slab") * tiles + lax.axis_index("tile")

    def cols(b):
        return pl.ds(pl.multiple_of(b * params, params), params)

    def fetch(b):
        return (
            pltpu.make_async_copy(prior_hbm.at[:, cols(b)], prior.at[:, cols(b)], prior_sems.at[b]),
            pltpu.make_async_copy(sens_hbm.at[b], sens.at[b], sens_sems.at[b]),
        )

    for b in range(depth):
        for copy in fetch(b):
            copy.start()

    def place(s, carry):
        storage[table[blocks, s]] = s ^ (me * owned)
        return carry

    lax.fori_loop(0, storage.shape[0], place, 0, unroll=8)
    acc[...] = jnp.zeros_like(acc)
    lane_group = lax.broadcasted_iota(jnp.int32, (obs_block, lanes), 1) // members_dev

    def work(b, carry):
        @pl.when(b + depth < blocks)
        def _():
            for copy in fetch(b + depth):
                copy.start()

        for copy in fetch(b):
            copy.wait()
        rows = prior[:, cols(b)].astype(jnp.bfloat16)
        bf_ref[:, cols(b)] = rows
        rows = jnp.concatenate([rows] * copies, axis=0)

        def add(count):
            terms = lax.dot_general(
                sens[b, : count * obs_block], rows, NT, preferred_element_type=jnp.float32
            )
            for k in range(count):
                block = table[b, k]
                at = storage[jnp.maximum(block, 0)]
                group = jnp.where(block >= 0, (at % owned) // groups, -1)
                acc[(at // owned) * groups + at % groups] += jnp.where(
                    lane_group == group, terms[k * obs_block : (k + 1) * obs_block], 0.0
                )

        counts = list(range(slots // 4, slots + 1, 4))
        for low, count in zip([0] + counts[:-1], counts):
            fits = (low == 0) | (table[b, low] >= 0)
            if count < slots:
                fits = fits & (table[b, count] < 0)
            pl.when(fits)(functools.partial(add, count))
        return carry

    lax.fori_loop(0, blocks, work, 0)

    def flush(r, carry):
        for g in range(groups):
            rows = slice(g * obs_block, (g + 1) * obs_block)
            keep_ref[r, rows, :] = acc[r * groups + g]
            send_ref[r, rows, :] = acc[(tiles + r) * groups + g]
        return carry

    lax.fori_loop(0, tiles, flush, 0, unroll=4)


def contribute(prior, sensitivity, pattern, ownership, perturbation):
    members_dev = prior.shape[0]
    blocks, slots, obs_block, params = sensitivity.shape
    tiles = lax.axis_size("tile")
    obs_dev = perturbation.shape[1]
    owned = obs_dev // obs_block
    lanes = 128
    groups = owned // (lanes // members_dev)
    half = jax.ShapeDtypeStruct((tiles, groups * obs_block, lanes), jnp.float32)
    total = ownership.shape[0]
    table = jnp.concatenate([jnp.pad(pattern, ((0, 0), (0, total - slots))), ownership[None]])
    hbm = pl.BlockSpec(memory_space=pl.ANY)
    return pl.pallas_call(
        functools.partial(contribute_kernel, owned, min(3, blocks), slots),
        in_specs=[SMEM, hbm, hbm],
        out_specs=[VMEM, VMEM, VMEM],
        out_shape=[
            half,
            half,
            jax.ShapeDtypeStruct((members_dev, prior.shape[1] + obs_dev), jnp.bfloat16),
        ],
        scratch_shapes=[
            pltpu.VMEM((blocks, slots * obs_block, params), jnp.bfloat16),
            pltpu.VMEM(prior.shape, jnp.float32),
            pltpu.VMEM((2 * tiles * groups, obs_block, lanes), jnp.float32),
            pltpu.SMEM(ownership.shape, jnp.int32),
            pltpu.SemaphoreType.DMA((blocks,)),
            pltpu.SemaphoreType.DMA((blocks,)),
        ],
        compiler_params=pltpu.CompilerParams(vmem_limit_bytes=54272 << 10),
        name="contribute",
    )(table, prior, sensitivity.reshape(blocks, slots * obs_block, params))


def gram_kernel(count, *refs):
    predicted, noise = refs[:count], refs[count : 2 * count]
    observed, sigma, keep, send, stack, whole = refs[2 * count :]
    members_dev = noise[0].shape[0]
    members = members_dev * count
    width, lanes = predicted[0].shape
    at = lax.axis_index("member")
    for r in range(count):
        rows = pl.ds(pl.multiple_of((at ^ r) * members_dev, members_dev), members_dev)
        turned = predicted[r][...].T
        for q in range(lanes // members_dev):
            stack[rows, q * width : (q + 1) * width] = turned[
                q * members_dev : (q + 1) * members_dev
            ]
        whole_rows = pl.ds(pl.multiple_of(members + (at ^ r) * members_dev, members_dev), members_dev)
        stack[whole_rows, :] = noise[r][:, -stack.shape[1] :].astype(jnp.float32)
    values = stack[:members, :]
    inverse = 1.0 / sigma[...]
    spread = (values - jnp.mean(values, axis=0, keepdims=True)) * (
        inverse * (1.0 / math.sqrt(members - 1))
    )
    innovation = (observed[...] - values) * inverse + stack[members:, :]
    stack[:members, :] = spread
    stack[members:, :] = innovation
    misfit = jnp.sum(jnp.sum(innovation * innovation, axis=0, keepdims=True), axis=1, keepdims=True)
    both = lax.dot_general(
        spread, stack[...], NT, precision=EXACT, preferred_element_type=jnp.float32
    )
    row = lax.broadcasted_iota(jnp.int32, both.shape, 0)
    col = lax.broadcasted_iota(jnp.int32, both.shape, 1)
    both = both + jnp.where(row == col, misfit * (1.0 / (4.0 * members * members)), 0.0)
    system, cross = both[:, :members], both[:, members:]
    half = members // 2
    first, last = system[:half, :half], system[half:, half:]
    above = row[:half, :half] <= col[:half, :half]
    whole[: members, :] = cross
    whole[members : members + half, :half] = system[:half, half:]
    whole[members : members + half, half:] = jnp.where(above, first, last)
    diagonal = jnp.sum(jnp.where(row == col, both, 0.0)[:, :members], axis=0, keepdims=True)
    side = lax.axis_index("slab")
    for out, at in ((keep, side), (send, 1 - side)):
        out[:half, :] = whole[pl.ds(pl.multiple_of(at * half, half), half), :]
        quarter = half // 2
        out[half : half + quarter, :] = whole[
            pl.ds(pl.multiple_of(members + at * quarter, quarter), quarter), :
        ]
        out[half + quarter :, :] = jnp.broadcast_to(diagonal, (8, members))


def gram(predicted, noise, observed, sigma):
    count = len(predicted)
    members_dev, obs_dev = noise[0].shape[0], observed.shape[0]
    members = members_dev * count
    half = jax.ShapeDtypeStruct((members // 2 + members // 4 + 8, members), jnp.float32)
    return pl.pallas_call(
        functools.partial(gram_kernel, count),
        in_specs=[VMEM] * (2 * count + 2),
        out_specs=[VMEM, VMEM],
        out_shape=[half, half],
        scratch_shapes=[
            pltpu.VMEM((2 * members, obs_dev), jnp.float32),
            pltpu.VMEM((members + members // 2, members), jnp.float32),
        ],
        compiler_params=pltpu.CompilerParams(vmem_limit_bytes=8 << 20),
        name="gram",
    )(*predicted, *noise, observed.reshape(1, obs_dev), sigma.reshape(1, obs_dev))


def update_kernel(count, *refs):
    mine, other = refs[:2]
    prior = refs[2 : 2 + count]
    increment, weights, cross, packed, cols, ensemble, _, _ = refs[2 + count :]
    members = weights.shape[0]
    members_dev = members // count
    at = lax.axis_index("member")
    side = lax.axis_index("slab")
    own_rows = pl.ds(pl.multiple_of(at * members_dev, members_dev), members_dev)
    for r in range(count):
        rows = pl.ds(pl.multiple_of((at ^ r) * members_dev, members_dev), members_dev)
        ensemble[rows, :] = prior[r][:, : ensemble.shape[1]]
    half, quarter = members // 2, members // 4
    for part, at_side in ((mine, side), (other, 1 - side)):
        cross[pl.ds(pl.multiple_of(at_side * half, half), half), :] = part[:half, :]
        packed[pl.ds(pl.multiple_of(at_side * quarter, quarter), quarter), :] = part[
            half : half + quarter, :
        ]
    row = lax.broadcasted_iota(jnp.int32, (members, members), 0)
    col = lax.broadcasted_iota(jnp.int32, (members, members), 1)
    eye = jnp.where(row == col, 1.0, 0.0)
    top = packed[...]
    turned = top.T
    mixed, mixed_turned = top[:, half:], turned[half:, :]
    above = row[:half, :half] <= col[:half, :half]
    system = jnp.concatenate(
        [
            jnp.concatenate([jnp.where(above, mixed, mixed_turned), top[:, :half]], axis=1),
            jnp.concatenate([turned[:half, :], jnp.where(above, mixed_turned, mixed)], axis=1),
        ],
        axis=0,
    )
    system = jnp.where(row == col, mine[half + quarter : half + quarter + 1, :], system)

    def total(x):
        return jnp.sum(jnp.sum(x, axis=0, keepdims=True), axis=1, keepdims=True)

    trace = total(system * eye)
    system = system + (trace - total(system)) * (1.0 / (members * members))
    bound = jnp.max(jnp.sum(jnp.abs(system), axis=0, keepdims=True), axis=1, keepdims=True)

    def begin(scale):
        return eye - scale * system, cross[...] * scale

    power, terms = begin(total(system * eye) / total(system * system))

    def step(power, terms):
        pair = lax.dot_general(
            power,
            jnp.concatenate([power, terms], axis=1),
            (((1,), (0,)), ((), ())),
            precision=EXACT,
            preferred_element_type=jnp.float32,
        )
        return pair[:, :members], terms + pair[:, members:]

    for _ in range(4):
        power, terms = step(power, terms)

    def unfinished(carry):
        power, _, count = carry
        return (jnp.sum(power * power) > 1e-12) & (count < 40)

    def further(carry):
        power, terms, count = carry
        power, terms = step(power, terms)
        return power, terms, count + 1

    shrinks = jnp.sum(power * power, axis=0, keepdims=True)
    shrinks = jnp.sum(shrinks, axis=1, keepdims=True) < 1.0
    sure_power, sure_terms = begin(1.9 / bound)
    power = jnp.where(shrinks, power, sure_power)
    terms = jnp.where(shrinks, terms, sure_terms)
    _, terms, _ = lax.while_loop(unfinished, further, (power, terms, 0))
    weights[...] = terms
    centred = (terms - jnp.mean(terms, axis=0, keepdims=True)) * (1.0 / math.sqrt(members - 1))
    cols[...] = centred.T
    own = cols[own_rows, :].astype(jnp.bfloat16)
    for n in range(4):
        lanes = pl.ds(n * 1024, 1024)
        increment[:, lanes] = jnp.dot(own, ensemble[:, lanes], preferred_element_type=jnp.float32)


def update(mine, other, prior, params):
    count = len(prior)
    members_dev = prior[0].shape[0]
    members = members_dev * count
    return pl.pallas_call(
        functools.partial(update_kernel, count),
        in_specs=[VMEM] * (2 + count),
        out_specs=[VMEM, VMEM],
        out_shape=[
            jax.ShapeDtypeStruct((members_dev, params), jnp.float32),
            jax.ShapeDtypeStruct((members, members), jnp.float32),
        ],
        scratch_shapes=[
            pltpu.VMEM((members, members), jnp.float32),
            pltpu.VMEM((members // 2, members), jnp.float32),
            pltpu.VMEM((members, members), jnp.float32),
            pltpu.VMEM((members, params), jnp.bfloat16),
            pltpu.VMEM((members_dev, params), jnp.float32),
            pltpu.SemaphoreType.DMA((4,)),
        ],
        compiler_params=pltpu.CompilerParams(vmem_limit_bytes=8 << 20),
        name="update",
    )(mine, other, *prior)


def step(prior, sensitivity, pattern, ownership, observed, obs_noise, perturbation):
    tiles = lax.axis_size("tile")
    keep, send, own = contribute(prior, sensitivity, pattern, ownership, perturbation)
    own = lax.dynamic_update_slice(own, perturbation.astype(own.dtype), (0, prior.shape[1]))
    got = swap(send, "slab", 1)
    chunks = [keep[r] + got[r] for r in range(tiles)]
    ensemble = gather_xor(own, "member")
    for shift, radix in digits(tiles):
        low = 1 << shift
        arrived = [
            [swap(chunks[d * low + r], "tile", d << shift) for r in range(low)]
            for d in range(1, radix)
        ]
        chunks = [sum((g[r] for g in arrived), chunks[r]) for r in range(low)]
    predicted = gather_xor(chunks[0], "member")
    keep, send = gram(predicted, ensemble, observed, obs_noise)
    mine = keep + swap(send, "slab", 1)
    for shift, radix in digits(tiles)[::-1]:
        mine = sum((swap(mine, "tile", d << shift) for d in range(1, radix)), mine)
    return tuple(update(mine, swap(mine, "slab", 1), ensemble, prior.shape[1]))


def solution(mesh):
    return jax.shard_map(
        step,
        mesh=mesh,
        in_specs=(
            P("member", ("slab", "tile")),
            P(("slab", "tile"), None, None, None),
            P(("slab", "tile"), None),
            P(),
            P(("slab", "tile")),
            P(("slab", "tile")),
            P("member", ("slab", "tile")),
        ),
        out_specs=(P("member", ("slab", "tile")), P()),
        check_vma=False,
    )
```

```python
import functools
import math

import jax
import jax.numpy as jnp
from jax import lax
from jax.experimental import pallas as pl
from jax.experimental.pallas import tpu as pltpu
from jax.sharding import PartitionSpec as P


EXACT = lax.Precision.HIGHEST
VMEM = pl.BlockSpec(memory_space=pltpu.VMEM)
SMEM = pl.BlockSpec(memory_space=pltpu.SMEM)
NT = (((1,), (1,)), ((), ()))


def swap(x, axis, distance):
    size = lax.axis_size(axis)
    return lax.ppermute(x, axis, [(i, i ^ distance) for i in range(size)])


def digits(size):
    out, shift = [], 0
    while size > 1:
        radix = 4 if size % 4 == 0 else 2
        out.append((shift, radix))
        shift += radix.bit_length() - 1
        size //= radix
    return out[::-1]


def gather_xor(x, axis):
    return [x] + [swap(x, axis, r) for r in range(1, lax.axis_size(axis))]


def contribute_kernel(
    owned,
    depth,
    slots,
    table,
    prior_hbm,
    sens_hbm,
    keep_ref,
    send_ref,
    bf_ref,
    sens,
    prior,
    acc,
    storage,
    sens_sems,
    prior_sems,
):
    blocks = sens.shape[0]
    tiles, _, lanes = keep_ref.shape
    members_dev = prior.shape[0]
    _, rows_block, params = sens.shape
    obs_block = rows_block // slots
    copies = lanes // members_dev
    groups = owned // copies
    me = lax.axis_index("slab") * tiles + lax.axis_index("tile")

    def cols(b):
        return pl.ds(pl.multiple_of(b * params, params), params)

    def fetch(b):
        return (
            pltpu.make_async_copy(prior_hbm.at[:, cols(b)], prior.at[:, cols(b)], prior_sems.at[b]),
            pltpu.make_async_copy(sens_hbm.at[b], sens.at[b], sens_sems.at[b]),
        )

    for b in range(depth):
        for copy in fetch(b):
            copy.start()

    def place(s, carry):
        storage[table[blocks, s]] = s ^ (me * owned)
        return carry

    lax.fori_loop(0, storage.shape[0], place, 0, unroll=8)
    acc[...] = jnp.zeros_like(acc)
    lane_group = lax.broadcasted_iota(jnp.int32, (obs_block, lanes), 1) // members_dev

    def work(b, carry):
        @pl.when(b + depth < blocks)
        def _():
            for copy in fetch(b + depth):
                copy.start()

        for copy in fetch(b):
            copy.wait()
        rows = prior[:, cols(b)].astype(jnp.bfloat16)
        bf_ref[:, cols(b)] = rows
        rows = jnp.concatenate([rows] * copies, axis=0)

        def add(count):
            terms = lax.dot_general(
                sens[b, : count * obs_block], rows, NT, preferred_element_type=jnp.float32
            )
            for k in range(count):
                block = table[b, k]
                at = storage[jnp.maximum(block, 0)]
                group = jnp.where(block >= 0, (at % owned) // groups, -1)
                acc[(at // owned) * groups + at % groups] += jnp.where(
                    lane_group == group, terms[k * obs_block : (k + 1) * obs_block], 0.0
                )

        counts = list(range(slots // 4, slots + 1, 4))
        for low, count in zip([0] + counts[:-1], counts):
            fits = (low == 0) | (table[b, low] >= 0)
            if count < slots:
                fits = fits & (table[b, count] < 0)
            pl.when(fits)(functools.partial(add, count))
        return carry

    lax.fori_loop(0, blocks, work, 0)

    def flush(r, carry):
        for g in range(groups):
            rows = slice(g * obs_block, (g + 1) * obs_block)
            keep_ref[r, rows, :] = acc[r * groups + g]
            send_ref[r, rows, :] = acc[(tiles + r) * groups + g]
        return carry

    lax.fori_loop(0, tiles, flush, 0, unroll=4)


def contribute(prior, sensitivity, pattern, ownership, perturbation):
    members_dev = prior.shape[0]
    blocks, slots, obs_block, params = sensitivity.shape
    tiles = lax.axis_size("tile")
    obs_dev = perturbation.shape[1]
    owned = obs_dev // obs_block
    lanes = 128
    groups = owned // (lanes // members_dev)
    half = jax.ShapeDtypeStruct((tiles, groups * obs_block, lanes), jnp.float32)
    total = ownership.shape[0]
    table = jnp.concatenate([jnp.pad(pattern, ((0, 0), (0, total - slots))), ownership[None]])
    hbm = pl.BlockSpec(memory_space=pl.ANY)
    return pl.pallas_call(
        functools.partial(contribute_kernel, owned, min(4, blocks), slots),
        in_specs=[SMEM, hbm, hbm],
        out_specs=[VMEM, VMEM, VMEM],
        out_shape=[
            half,
            half,
            jax.ShapeDtypeStruct((members_dev, prior.shape[1] + obs_dev), jnp.bfloat16),
        ],
        scratch_shapes=[
            pltpu.VMEM((blocks, slots * obs_block, params), jnp.bfloat16),
            pltpu.VMEM(prior.shape, jnp.float32),
            pltpu.VMEM((2 * tiles * groups, obs_block, lanes), jnp.float32),
            pltpu.SMEM(ownership.shape, jnp.int32),
            pltpu.SemaphoreType.DMA((blocks,)),
            pltpu.SemaphoreType.DMA((blocks,)),
        ],
        compiler_params=pltpu.CompilerParams(vmem_limit_bytes=54272 << 10),
        name="contribute",
    )(table, prior, sensitivity.reshape(blocks, slots * obs_block, params))


def gram_kernel(count, *refs):
    predicted, noise = refs[:count], refs[count : 2 * count]
    observed, sigma, keep, send, stack, whole = refs[2 * count :]
    members_dev = noise[0].shape[0]
    members = members_dev * count
    width, lanes = predicted[0].shape
    at = lax.axis_index("member")
    for r in range(count):
        rows = pl.ds(pl.multiple_of((at ^ r) * members_dev, members_dev), members_dev)
        turned = predicted[r][...].T
        for q in range(lanes // members_dev):
            stack[rows, q * width : (q + 1) * width] = turned[
                q * members_dev : (q + 1) * members_dev
            ]
        whole_rows = pl.ds(pl.multiple_of(members + (at ^ r) * members_dev, members_dev), members_dev)
        stack[whole_rows, :] = noise[r][:, -stack.shape[1] :].astype(jnp.float32)
    values = stack[:members, :]
    inverse = 1.0 / sigma[...]
    spread = (values - jnp.mean(values, axis=0, keepdims=True)) * (
        inverse * (1.0 / math.sqrt(members - 1))
    )
    innovation = (observed[...] - values) * inverse + stack[members:, :]
    stack[:members, :] = spread
    stack[members:, :] = innovation
    misfit = jnp.sum(jnp.sum(innovation * innovation, axis=0, keepdims=True), axis=1, keepdims=True)
    both = lax.dot_general(
        spread, stack[...], NT, precision=EXACT, preferred_element_type=jnp.float32
    )
    row = lax.broadcasted_iota(jnp.int32, both.shape, 0)
    col = lax.broadcasted_iota(jnp.int32, both.shape, 1)
    both = both + jnp.where(row == col, misfit * (1.0 / (4.0 * members * members)), 0.0)
    system, cross = both[:, :members], both[:, members:]
    half = members // 2
    first, last = system[:half, :half], system[half:, half:]
    above = row[:half, :half] <= col[:half, :half]
    whole[: members, :] = cross
    whole[members : members + half, :half] = system[:half, half:]
    whole[members : members + half, half:] = jnp.where(above, first, last)
    diagonal = jnp.sum(jnp.where(row == col, both, 0.0)[:, :members], axis=0, keepdims=True)
    side = lax.axis_index("slab")
    for out, at in ((keep, side), (send, 1 - side)):
        out[:half, :] = whole[pl.ds(pl.multiple_of(at * half, half), half), :]
        quarter = half // 2
        out[half : half + quarter, :] = whole[
            pl.ds(pl.multiple_of(members + at * quarter, quarter), quarter), :
        ]
        out[half + quarter :, :] = jnp.broadcast_to(diagonal, (8, members))


def gram(predicted, noise, observed, sigma):
    count = len(predicted)
    members_dev, obs_dev = noise[0].shape[0], observed.shape[0]
    members = members_dev * count
    half = jax.ShapeDtypeStruct((members // 2 + members // 4 + 8, members), jnp.float32)
    return pl.pallas_call(
        functools.partial(gram_kernel, count),
        in_specs=[VMEM] * (2 * count + 2),
        out_specs=[VMEM, VMEM],
        out_shape=[half, half],
        scratch_shapes=[
            pltpu.VMEM((2 * members, obs_dev), jnp.float32),
            pltpu.VMEM((members + members // 2, members), jnp.float32),
        ],
        compiler_params=pltpu.CompilerParams(vmem_limit_bytes=8 << 20),
        name="gram",
    )(*predicted, *noise, observed.reshape(1, obs_dev), sigma.reshape(1, obs_dev))


def update_kernel(count, *refs):
    mine, other = refs[:2]
    prior, late = refs[2 : 2 + count], refs[2 + count]
    increment, weights, cross, packed, cols, ensemble, _, _ = refs[3 + count :]
    members = weights.shape[0]
    members_dev = members // count
    at = lax.axis_index("member")
    side = lax.axis_index("slab")
    own_rows = pl.ds(pl.multiple_of(at * members_dev, members_dev), members_dev)
    for r in range(count):
        rows = pl.ds(pl.multiple_of((at ^ r) * members_dev, members_dev), members_dev)
        cut = late.shape[1] if r == count - 1 else 0
        ensemble[rows, cut:] = prior[r][:, : ensemble.shape[1] - cut]
        if cut:
            ensemble[rows, :cut] = late[...]
    half, quarter = members // 2, members // 4
    for part, at_side in ((mine, side), (other, 1 - side)):
        cross[pl.ds(pl.multiple_of(at_side * half, half), half), :] = part[:half, :]
        packed[pl.ds(pl.multiple_of(at_side * quarter, quarter), quarter), :] = part[
            half : half + quarter, :
        ]
    row = lax.broadcasted_iota(jnp.int32, (members, members), 0)
    col = lax.broadcasted_iota(jnp.int32, (members, members), 1)
    eye = jnp.where(row == col, 1.0, 0.0)
    top = packed[...]
    turned = top.T
    mixed, mixed_turned = top[:, half:], turned[half:, :]
    above = row[:half, :half] <= col[:half, :half]
    system = jnp.concatenate(
        [
            jnp.concatenate([jnp.where(above, mixed, mixed_turned), top[:, :half]], axis=1),
            jnp.concatenate([turned[:half, :], jnp.where(above, mixed_turned, mixed)], axis=1),
        ],
        axis=0,
    )
    system = jnp.where(row == col, mine[half + quarter : half + quarter + 1, :], system)

    def total(x):
        return jnp.sum(jnp.sum(x, axis=0, keepdims=True), axis=1, keepdims=True)

    trace, entries, squares = total(system * eye), total(system), total(system * system)
    shift = (trace - entries) * (1.0 / (members * members))
    system = system + shift
    trace = trace + members * shift
    squares = squares + shift * (2.0 * entries + (members * members) * shift)

    def begin(scale):
        return eye - scale * system, cross[...] * scale

    def apply(power, terms):
        return lax.dot_general(
            power,
            terms,
            (((1,), (0,)), ((), ())),
            precision=EXACT,
            preferred_element_type=jnp.float32,
        )

    def step(power, terms):
        pair = apply(power, jnp.concatenate([power, terms], axis=1))
        return pair[:, :members], terms + pair[:, members:]

    power, terms = begin(trace / squares)
    for _ in range(3):
        power, terms = step(power, terms)
    solved = terms + apply(power, terms)

    def unfinished(carry):
        power, _, _, count = carry
        return jnp.logical_not(jnp.sum(power * power) <= 1e-6) & (count < 40)

    def further(carry):
        power, terms, _, count = carry
        bound = jnp.max(jnp.sum(jnp.abs(system), axis=0, keepdims=True), axis=1, keepdims=True)
        sure_power, sure_terms = begin(1.9 / bound)
        shrinks = total(power * power) < 1.0
        again = jnp.logical_not(shrinks) & (count == 0)
        power = jnp.where(again, sure_power, power)
        terms = jnp.where(again, sure_terms, terms)
        power, terms = step(power, terms)
        return power, terms, terms + apply(power, terms), count + 1

    terms = lax.while_loop(unfinished, further, (power, terms, solved, 0))[2]
    weights[...] = terms
    centred = (terms - jnp.mean(terms, axis=0, keepdims=True)) * (1.0 / math.sqrt(members - 1))
    cols[...] = centred.T
    own = cols[own_rows, :].astype(jnp.bfloat16)
    for n in range(4):
        lanes = pl.ds(n * 1024, 1024)
        increment[:, lanes] = jnp.dot(own, ensemble[:, lanes], preferred_element_type=jnp.float32)


def update(mine, other, prior, late, params):
    count = len(prior)
    members_dev = prior[0].shape[0]
    members = members_dev * count
    return pl.pallas_call(
        functools.partial(update_kernel, count),
        in_specs=[VMEM] * (3 + count),
        out_specs=[VMEM, VMEM],
        out_shape=[
            jax.ShapeDtypeStruct((members_dev, params), jnp.float32),
            jax.ShapeDtypeStruct((members, members), jnp.float32),
        ],
        scratch_shapes=[
            pltpu.VMEM((members, members), jnp.float32),
            pltpu.VMEM((members // 2, members), jnp.float32),
            pltpu.VMEM((members, members), jnp.float32),
            pltpu.VMEM((members, params), jnp.bfloat16),
            pltpu.VMEM((members_dev, params), jnp.float32),
            pltpu.SemaphoreType.DMA((4,)),
        ],
        compiler_params=pltpu.CompilerParams(vmem_limit_bytes=8 << 20),
        name="update",
    )(mine, other, *prior, late)


def step(prior, sensitivity, pattern, ownership, observed, obs_noise, perturbation):
    tiles = lax.axis_size("tile")
    keep, send, own = contribute(prior, sensitivity, pattern, ownership, perturbation)
    own = lax.dynamic_update_slice(own, perturbation.astype(own.dtype), (0, prior.shape[1]))
    got = swap(send, "slab", 1)
    chunks = [keep[r] + got[r] for r in range(tiles)]
    last, cut = lax.axis_size("member") - 1, prior.shape[1] // 4
    ensemble = [own] + [swap(own, "member", r) for r in range(1, last)]
    ensemble.append(swap(own[:, cut:], "member", last))
    late = swap(own[:, :cut], "member", last)
    for shift, radix in digits(tiles):
        low = 1 << shift
        arrived = [
            [swap(chunks[d * low + r], "tile", d << shift) for r in range(low)]
            for d in range(1, radix)
        ]
        chunks = [sum((g[r] for g in arrived), chunks[r]) for r in range(low)]
    predicted = gather_xor(chunks[0], "member")
    keep, send = gram(predicted, ensemble, observed, obs_noise)
    mine = keep + swap(send, "slab", 1)
    for shift, radix in digits(tiles)[::-1]:
        mine = sum((swap(mine, "tile", d << shift) for d in range(1, radix)), mine)
    return tuple(update(mine, swap(mine, "slab", 1), ensemble, late, prior.shape[1]))


def solution(mesh):
    return jax.shard_map(
        step,
        mesh=mesh,
        in_specs=(
            P("member", ("slab", "tile")),
            P(("slab", "tile"), None, None, None),
            P(("slab", "tile"), None),
            P(),
            P(("slab", "tile")),
            P(("slab", "tile")),
            P("member", ("slab", "tile")),
        ),
        out_specs=(P("member", ("slab", "tile")), P()),
        check_vma=False,
    )
```
